512 devices in a mesh: dp: 32 (over z, x), rows: 16 (over y, core).
Axes of the slice: x: 4, y: 8, z: 8, core: 2. Of those that a mesh axis runs over, the one named last changes fastest.
Arguments:
- older_output: bfloat16 [7680, 12, 2048], P(('dp', 'rows')), parts along dimension 0, may hold values from -6 to 6
- newer_output: bfloat16 [7680, 12, 2048], P(('dp', 'rows')), parts along dimension 0, may hold values from -6 to 6
- output_grad: bfloat16 [7680, 12, 2048], P(('dp', 'rows')), parts along dimension 0, may hold values from -6 to 6
- older_weight: bfloat16 [2048, 512], P('rows'), may hold values from -0.1875 to 0.1875
- newer_weight: bfloat16 [2048, 512], P('rows'), may hold values from -0.1875 to 0.1875
- square_point: bfloat16 [512, 512], P('rows'), may hold values from -0.25 to 0.25
- column_point: bfloat16 [512, 512], P('rows'), may hold values from -0.25 to 0.25
- square_kernel: float32 [3, 3, 512], replicated, may hold values from -2.4 to 2.4
- column_kernel: float32 [7, 512], replicated, may hold values from -2.4 to 2.4
Outputs:
- cell_output: bfloat16 [7680, 12, 2048], P(('dp', 'rows')), parts along dimension 0
- older_grad: bfloat16 [7680, 12, 2048], P(('dp', 'rows')), parts along dimension 0
- newer_grad: bfloat16 [7680, 12, 2048], P(('dp', 'rows')), parts along dimension 0
The draws below stay inside these ranges and needn't reach their ends.
There are 32 independent parts, one for each index of `dp`. The reference program is written for one: setup_inputs(seed, part) draws one part's arguments, and reference() takes and returns one part's arrays. A program takes and returns all parts, laid end to end along the dimension named above; an argument that names none is the same for every part. Nothing has to cross between parts.
All inputs are finite; a program needn't handle non-finite values.
Results may differ from the reference program's by a relative error of at most 0.0057.
Values may be sent and summed in bfloat16 or wider, within the bound.
No kernel may reach another device: no remote copies, remote signals or barrier semaphores. Data moves between devices by JAX's collectives and lax.ppermute only.
A program may use at most 64 MiB of HBM per device.

```python
import jax
import jax.numpy as jnp

C = 512
CIN = 2048
IMGS = 8
HEIGHT = 30
WIDE = 12
OUTC = 2048


def steps_of(own_key, shape, cuts, least, largest):
    def one(dim, blocks):
        heights = jax.random.uniform(jax.random.fold_in(jax.random.fold_in(own_key, 6), dim), (blocks,), jnp.float32, least / len(cuts), largest / len(cuts))
        return jnp.repeat(jnp.exp(heights), shape[dim] // blocks).reshape((-1,) + (1,) * (len(shape) - dim - 1))

    loudness = one(*cuts[0])
    for cut in cuts[1:]:
        loudness = loudness * one(*cut)
    return loudness


def normal_values(key, extent, deviation, bound, pieces=(), kind=jnp.bfloat16):
    factor_of = steps_of(key, extent, pieces, -0.22, 0.18) if pieces else 1.0
    drawn = jax.random.normal(key, extent, jnp.float32) * deviation * factor_of
    return jnp.minimum(jnp.maximum(drawn, -bound), bound).astype(kind)


def setup_inputs(seed: int = 0, part: int = 0) -> dict:
    splits = jax.random.split(jax.random.key(seed), 10)
    part_keys = jax.random.split(jax.random.fold_in(splits[9], part), 10)
    return {
        "older_output": normal_values(part_keys[0], (IMGS * HEIGHT, WIDE, CIN), 1.0, 6.0, ((0, 16),)),
        "newer_output": normal_values(part_keys[1], (IMGS * HEIGHT, WIDE, CIN), 1.0, 6.0, ((0, 16),)),
        "output_grad": normal_values(part_keys[2], (IMGS * HEIGHT, WIDE, OUTC), 1.0, 6.0, ((0, 16),)),
        "older_weight": normal_values(splits[3], (CIN, C), (CIN // 2) ** -0.5, 0.1875, ((0, 16),)),
        "newer_weight": normal_values(splits[4], (CIN, C), (CIN // 2) ** -0.5, 0.1875, ((0, 16),)),
        "square_point": normal_values(splits[5], (C, C), C ** -0.5, 0.25, ((0, 16),)),
        "column_point": normal_values(splits[6], (C, C), C ** -0.5, 0.25, ((0, 16),)),
        "square_kernel": normal_values(splits[7], (3, 3, C), 0.4, 2.4, (), jnp.float32),
        "column_kernel": normal_values(splits[8], (7, C), 0.4, 2.4, (), jnp.float32),
    }


def rows_pad(field, width):
    return jnp.pad(field, ((0, 0), (width, width), (0, 0), (0, 0)))


def square_taps(padded, kernel, flip):
    full = jnp.pad(padded, ((0, 0), (0, 0), (1, 1), (0, 0))).astype(jnp.float32)
    height = full.shape[1] - 2
    across = full.shape[2] - 2
    total = jnp.zeros((full.shape[0], height, across, full.shape[3]), jnp.float32)
    for i in range(3):
        for j in range(3):
            first = 2 - i if flip else i
            second = 2 - j if flip else j
            total = total + full[:, first:first + height, second:second + across, :] * kernel[i, j]
    return total


def column_taps(padded, kernel, flip):
    full = padded.astype(jnp.float32)
    height = full.shape[1] - 6
    total = jnp.zeros((full.shape[0], height, full.shape[2], full.shape[3]), jnp.float32)
    for i in range(7):
        first = 6 - i if flip else i
        total = total + full[:, first:first + height, :, :] * kernel[i]
    return total


def reference(older_output, newer_output, output_grad, older_weight, newer_weight, square_point, column_point, square_kernel, column_kernel):
    stacked, across, channels = older_output.shape
    images = IMGS
    height = HEIGHT
    filters = square_point.shape[0]
    shape_four = (images, height, across, filters)
    pool_kernel = jnp.full((3, 3, filters), 1.0 / 9.0, jnp.float32)
    older_flat = older_output.reshape(-1, channels)
    newer_flat = newer_output.reshape(-1, channels)
    older_mixed = jnp.dot(jnp.maximum(older_flat, 0), older_weight, preferred_element_type=jnp.float32).astype(jnp.bfloat16).reshape(shape_four)
    newer_mixed = jnp.dot(jnp.maximum(newer_flat, 0), newer_weight, preferred_element_type=jnp.float32).astype(jnp.bfloat16).reshape(shape_four)
    square_pre = square_taps(rows_pad(newer_mixed, 1), square_kernel, False).astype(jnp.bfloat16).reshape(-1, filters)
    column_pre = column_taps(rows_pad(older_mixed, 3), column_kernel, False).astype(jnp.bfloat16).reshape(-1, filters)
    pooled = square_taps(rows_pad(older_mixed, 1), pool_kernel, False).reshape(-1, filters)
    square_branch = jnp.dot(square_pre, square_point, preferred_element_type=jnp.float32)
    column_branch = jnp.dot(column_pre, column_point, preferred_element_type=jnp.float32)
    cell_output = jnp.concatenate([square_branch, column_branch, pooled, newer_mixed.reshape(-1, filters).astype(jnp.float32)], axis=1)
    cell_output = cell_output.astype(jnp.bfloat16).reshape(stacked, across, 4 * filters)
    grads = output_grad.reshape(-1, 4 * filters)
    grad_square = grads[:, :filters]
    grad_column = grads[:, filters:2 * filters]
    grad_pool = grads[:, 2 * filters:3 * filters].reshape(shape_four)
    grad_same = grads[:, 3 * filters:].reshape(shape_four)
    square_back = jnp.dot(grad_square, square_point.T, preferred_element_type=jnp.float32).astype(jnp.bfloat16).reshape(shape_four)
    column_back = jnp.dot(grad_column, column_point.T, preferred_element_type=jnp.float32).astype(jnp.bfloat16).reshape(shape_four)
    newer_back = (square_taps(rows_pad(square_back, 1), square_kernel, True) + grad_same.astype(jnp.float32)).astype(jnp.bfloat16)
    older_back = (column_taps(rows_pad(column_back, 3), column_kernel, True) + square_taps(rows_pad(grad_pool, 1), pool_kernel, True)).astype(jnp.bfloat16)
    older_mask = jnp.where(older_flat > 0, 1.0, 0.0).astype(jnp.float32)
    newer_mask = jnp.where(newer_flat > 0, 1.0, 0.0).astype(jnp.float32)
    older_grad = (jnp.dot(older_back.reshape(-1, filters), older_weight.T, preferred_element_type=jnp.float32) * older_mask).astype(jnp.bfloat16)
    newer_grad = (jnp.dot(newer_back.reshape(-1, filters), newer_weight.T, preferred_element_type=jnp.float32) * newer_mask).astype(jnp.bfloat16)
    return cell_output, older_grad.reshape(older_output.shape), newer_grad.reshape(newer_output.shape)
```

```python
import jax
import jax.numpy as jnp
from jax import lax
from jax.experimental import pallas as pl
from jax.experimental.pallas import tpu as pltpu
from jax.sharding import PartitionSpec as P

F32 = jnp.float32
BF16 = jnp.bfloat16
C = 512
CIN = 2048
WIDE = 12
ROWS = 15
LANES = 128
BLOCKS = C // LANES
PIECES = 4
SCALE = 2.0**17


def dot(a, b):
    return jnp.dot(a, b, preferred_element_type=F32)


def dot_t(a, b):
    return lax.dot_general(a, b, (((1,), (1,)), ((), ())), preferred_element_type=F32)


def halo_kernel(
    core_ref, xo_hbm, xn_hbm, g_hbm, wo_hbm, wn_hbm, ps_hbm, pc_hbm,
    xo_out, xn_out, g_out, h_out, w_out,
    raw, sems, weight_sems,
):
    first = core_ref[0] == 0
    turn = jnp.where(first, 1, 7)
    fields = ((xo_hbm, xo_out, True), (xn_hbm, xn_out, True), (g_hbm, g_out, False))
    copies = []
    for at, (src, _, _) in enumerate(fields):
        for q in range(PIECES):
            part = pl.ds(q * (WIDE // PIECES), WIDE // PIECES)
            copy = pltpu.make_async_copy(src.at[part], raw.at[at, part], sems.at[at, q])
            copy.start()
            copies.append(copy)
    row = 0
    loads = []
    for at, src in enumerate((wo_hbm, wn_hbm, ps_hbm, pc_hbm)):
        size = src.shape[0]
        copy = pltpu.make_async_copy(src, w_out.at[pl.ds(row, size)], weight_sems.at[at])
        copy.start()
        loads.append(copy)
        row += size
    for at, (_, dst, relu) in enumerate(fields):
        dst[:, 8:16, :] = jnp.zeros((WIDE, 8, CIN), BF16)
        for q in range(PIECES):
            copies[at * PIECES + q].wait()
        v = raw[at]
        dst[:, 0:ROWS, :] = jnp.maximum(v, 0) if relu else v
        sent = jnp.where(first, dst[:, 8:16, :].astype(F32), dst[:, 0:8, :].astype(F32))
        h_out[:, :, at * CIN : (at + 1) * CIN] = pltpu.roll(sent, turn, 1).astype(BF16)
    for copy in loads:
        copy.wait()


def cell_kernel(
    core_ref, xo_s, xn_s, g_s, h_ref, wo_ref, wn_ref, ps_ref, pc_ref, ks_ref, kc_ref,
    cell_hbm, og_hbm, ng_hbm,
    zo, zn, zs, zc, zp, cell_s, og_s, ng_s, sems,
):
    slot = lax.broadcasted_iota(jnp.int32, (1, 8, LANES), 1)
    first = core_ref[0] == 0
    above = jnp.where((slot >= 5) & jnp.logical_not(first), 1.0, 0.0).astype(F32)
    below = jnp.where((slot < 2) & first, 1.0, 0.0).astype(F32)
    edge = jnp.where((slot == 7) & first, 1.0, 0.0).astype(F32)

    for z in (zo, zn, zs, zp):
        z[:, 0] = jnp.zeros((BLOCKS, 32, LANES), F32)
        z[:, WIDE + 1] = jnp.zeros((BLOCKS, 32, LANES), F32)

    def fill(z, own, halo):
        own = own.astype(BF16).astype(F32).reshape(WIDE, 16, C)
        halo = halo.astype(BF16).astype(F32).reshape(WIDE, 8, C)
        for b in range(BLOCKS):
            o = own[:, :, b * LANES : (b + 1) * LANES]
            h = halo[:, :, b * LANES : (b + 1) * LANES]
            z[b, 1 : WIDE + 1, 0:8, :] = h * above
            z[b, 1 : WIDE + 1, 8:16, :] = o[:, 0:8]
            z[b, 1 : WIDE + 1, 16:24, :] = o[:, 8:16] + h * edge
            z[b, 1 : WIDE + 1, 24:32, :] = h * below

    def column(z, b, flip):
        acc = None
        for i in range(7):
            at = 5 + (6 - i if flip else i)
            k = kc_ref[i : i + 1, b * LANES : (b + 1) * LANES].reshape(1, 1, LANES)
            t = z[b, 1 : WIDE + 1, at : at + 16, :] * k
            acc = t if acc is None else acc + t
        return acc

    def square(z, b, flip):
        acc = None
        for i in range(3):
            at = 7 + (2 - i if flip else i)
            for j in range(3):
                w = 2 - j if flip else j
                k = ks_ref[i, j : j + 1, b * LANES : (b + 1) * LANES].reshape(1, 1, LANES)
                t = z[b, w : w + WIDE, at : at + 16, :] * k
                acc = t if acc is None else acc + t
        return acc

    def pool(z, b):
        rows = (
            z[b, :, 7 : 7 + 16, :] + z[b, :, 8 : 8 + 16, :] + z[b, :, 9 : 9 + 16, :]
        )
        return (rows[0:WIDE] + rows[1 : WIDE + 1] + rows[2 : WIDE + 2]) * (1.0 / 9.0)

    def gather(parts):
        return jnp.concatenate([p.astype(BF16).reshape(WIDE * 16, LANES) for p in parts], axis=1)

    copies = []

    def put(stage, hbm, j, value):
        stage[j] = value.astype(BF16).reshape(WIDE, 16, C)[:, 0:ROWS, :]
        copy = pltpu.make_async_copy(
            stage.at[j], hbm.at[:, :, pl.ds(j * C, C)], sems.at[len(copies)]
        )
        copy.start()
        copies.append(copy)

    def flat(ref, lo, hi):
        v = ref[:, :, lo:hi]
        return v.reshape(-1, hi - lo)

    ps = ps_ref[...]
    pc = pc_ref[...]
    fill(zs, dot_t(flat(g_s, 0, C), ps), dot_t(flat(h_ref, 2 * CIN, 2 * CIN + C), ps))
    fill(
        zc,
        dot_t(flat(g_s, C, 2 * C), pc),
        dot_t(flat(h_ref, 2 * CIN + C, 2 * CIN + 2 * C), pc),
    )
    fill(zp, flat(g_s, 2 * C, 3 * C), flat(h_ref, 2 * CIN + 2 * C, 2 * CIN + 3 * C))
    wo = wo_ref[...]
    wn = wn_ref[...]
    fill(zo, dot(flat(xo_s, 0, CIN), wo), dot(flat(h_ref, 0, CIN), wo))
    mixed = dot(flat(xn_s, 0, CIN), wn)
    fill(zn, mixed, dot(flat(h_ref, CIN, 2 * CIN), wn))
    put(cell_s, cell_hbm, 3, mixed)

    back = gather(
        [
            square(zs, b, True)
            + g_s[:, :, 3 * C + b * LANES : 3 * C + (b + 1) * LANES].astype(F32)
            for b in range(BLOCKS)
        ]
    )
    for j in range(4):
        term = dot_t(back, wn_ref[j * C : (j + 1) * C, :])
        put(ng_s, ng_hbm, j, jnp.where(flat(xn_s, j * C, (j + 1) * C).astype(F32) > 0, term, 0.0))
    back = gather([column(zc, b, True) + pool(zp, b) for b in range(BLOCKS)])
    for j in range(4):
        term = dot_t(back, wo_ref[j * C : (j + 1) * C, :])
        put(og_s, og_hbm, j, jnp.where(flat(xo_s, j * C, (j + 1) * C).astype(F32) > 0, term, 0.0))
    put(cell_s, cell_hbm, 0, dot(gather([square(zn, b, False) for b in range(BLOCKS)]), ps))
    put(cell_s, cell_hbm, 1, dot(gather([column(zo, b, False) for b in range(BLOCKS)]), pc))
    put(cell_s, cell_hbm, 2, gather([pool(zo, b) for b in range(BLOCKS)]))
    for copy in copies:
        copy.wait()


def placed(values, space):
    return [pltpu.with_memory_space_constraint(v, space) for v in values]


def run_halo(core, *operands):
    vmem = pl.BlockSpec(memory_space=pltpu.VMEM)
    hbm = pl.BlockSpec(memory_space=pltpu.HBM)
    padded = pltpu.VMEM((WIDE, 16, CIN), BF16)
    shards = sum(v.shape[0] for v in operands[3:])
    return pl.pallas_call(
        halo_kernel,
        out_shape=(padded,) * 3
        + (pltpu.VMEM((WIDE, 8, 3 * CIN), BF16), pltpu.VMEM((shards, C), BF16)),
        in_specs=[pl.BlockSpec(memory_space=pltpu.SMEM)] + [hbm] * 7,
        out_specs=(vmem,) * 5,
        scratch_shapes=[
            pltpu.VMEM((3, WIDE, ROWS, CIN), BF16),
            pltpu.SemaphoreType.DMA((3, PIECES)),
            pltpu.SemaphoreType.DMA((4,)),
        ],
        compiler_params=pltpu.CompilerParams(vmem_limit_bytes=16 * 1024 * 1024),
        name="halo",
    )(core, *placed(operands, pltpu.HBM))


def run_cell(core, *operands):
    vmem = pl.BlockSpec(memory_space=pltpu.VMEM)
    out = jax.ShapeDtypeStruct((WIDE, ROWS, CIN), BF16)
    field = pltpu.VMEM((BLOCKS, WIDE + 2, 32, LANES), F32)
    stage = pltpu.VMEM((4, WIDE, ROWS, C), BF16)
    return pl.pallas_call(
        cell_kernel,
        out_shape=(out, out, out),
        in_specs=[pl.BlockSpec(memory_space=pltpu.SMEM)] + [vmem] * 10,
        out_specs=(pl.BlockSpec(memory_space=pl.ANY),) * 3,
        scratch_shapes=[field] * 5 + [stage] * 3 + [pltpu.SemaphoreType.DMA((12,))],
        compiler_params=pltpu.CompilerParams(vmem_limit_bytes=24 * 1024 * 1024),
        name="cell",
    )(core, *placed(operands, pltpu.VMEM))


def local(
    older_output,
    newer_output,
    output_grad,
    older_weight,
    newer_weight,
    square_point,
    column_point,
    square_kernel,
    column_kernel,
):
    count = lax.axis_size("rows")
    core = lax.rem(lax.axis_index("rows"), 2)
    core = core.astype(jnp.int32).reshape(1)
    xo, xn, grad, rim, shard = run_halo(
        core,
        older_output.transpose(1, 0, 2),
        newer_output.transpose(1, 0, 2),
        output_grad.transpose(1, 0, 2),
        older_weight,
        newer_weight,
        square_point,
        column_point,
    )
    rim = lax.ppermute(rim, "rows", [(i, i ^ 1) for i in range(count)])
    shard = (shard * jnp.asarray(SCALE, BF16)).astype(jnp.float16)
    full = lax.all_gather(shard, "rows", axis=0, tiled=False)

    def part(lo, hi):
        piece = (full[:, lo:hi].astype(F32) * (1.0 / SCALE)).astype(BF16)
        return piece.reshape(-1, C)

    k = older_weight.shape[0]
    p = square_point.shape[0]
    cell, og, ng = run_cell(
        core,
        xo,
        xn,
        grad,
        rim,
        part(0, k),
        part(k, 2 * k),
        part(2 * k, 2 * k + p),
        part(2 * k + p, 2 * k + 2 * p),
        square_kernel,
        column_kernel,
    )
    return cell.transpose(1, 0, 2), og.transpose(1, 0, 2), ng.transpose(1, 0, 2)


def solution(mesh):
    rows = P(("dp", "rows"), None, None)
    in_specs = (rows, rows, rows) + (P("rows", None),) * 4 + (P(), P())
    return jax.shard_map(
        local, mesh=mesh, in_specs=in_specs, out_specs=(rows,) * 3, check_vma=False
    )
```

```python
import jax
import jax.numpy as jnp
from jax import lax
from jax.experimental import pallas as pl
from jax.experimental.pallas import tpu as pltpu
from jax.sharding import PartitionSpec as P

F32 = jnp.float32
BF16 = jnp.bfloat16
C = 512
CIN = 2048
WIDE = 12
ROWS = 15
LANES = 128
BLOCKS = C // LANES
PIECES = 4
SCALE = 2.0**17
UNSCALE = 1.0 / SCALE


def dot(a, b):
    return jnp.dot(a, b, preferred_element_type=F32)


def dot_t(a, b):
    return lax.dot_general(a, b, (((1,), (1,)), ((), ())), preferred_element_type=F32)


def halo_kernel(
    core_ref, xo_hbm, xn_hbm, g_hbm, wo_hbm, wn_hbm, ps_hbm, pc_hbm,
    xo_out, xn_out, g_out, h_out, w_out,
    raw, sems, weight_sems,
):
    first = core_ref[0] == 0
    turn = jnp.where(first, 1, 7)
    fields = ((xo_hbm, xo_out, True), (xn_hbm, xn_out, True), (g_hbm, g_out, False))
    copies = []
    for at, (src, _, _) in enumerate(fields):
        for q in range(PIECES):
            part = pl.ds(q * (WIDE // PIECES), WIDE // PIECES)
            copy = pltpu.make_async_copy(src.at[part], raw.at[at, part], sems.at[at, q])
            copy.start()
            copies.append(copy)
    row = 0
    loads = []
    for at, src in enumerate((wo_hbm, wn_hbm, ps_hbm, pc_hbm)):
        size = src.shape[0]
        copy = pltpu.make_async_copy(src, w_out.at[pl.ds(row, size)], weight_sems.at[at])
        copy.start()
        loads.append(copy)
        row += size
    for at, (_, dst, relu) in enumerate(fields):
        dst[:, 8:16, :] = jnp.zeros((WIDE, 8, CIN), BF16)
        for q in range(PIECES):
            copies[at * PIECES + q].wait()
        v = raw[at]
        dst[:, 0:ROWS, :] = jnp.maximum(v, 0) if relu else v
        sent = jnp.where(first, dst[:, 8:16, :].astype(F32), dst[:, 0:8, :].astype(F32))
        h_out[:, :, at * CIN : (at + 1) * CIN] = pltpu.roll(sent, turn, 1).astype(BF16)
    for copy in loads:
        copy.wait()


def cell_kernel(
    core_ref, xo_s, xn_s, g_s, h_ref, wo_ref, wn_ref, ps_ref, pc_ref, ks_ref, kc_ref,
    cell_hbm, og_hbm, ng_hbm,
    zo, zn, zs, zc, zp, cell_s, og_s, ng_s, sems,
):
    slot = lax.broadcasted_iota(jnp.int32, (1, 8, LANES), 1)
    first = core_ref[0] == 0
    above = jnp.where((slot >= 5) & jnp.logical_not(first), 1.0, 0.0).astype(F32)
    below = jnp.where((slot < 2) & first, 1.0, 0.0).astype(F32)
    edge = jnp.where((slot == 7) & first, 1.0, 0.0).astype(F32)

    for z in (zo, zn, zs, zp):
        z[:, 0] = jnp.zeros((BLOCKS, 32, LANES), F32)
        z[:, WIDE + 1] = jnp.zeros((BLOCKS, 32, LANES), F32)

    def fill(z, own, halo):
        own = own.astype(BF16).astype(F32).reshape(WIDE, 16, -1)
        halo = halo.astype(BF16).astype(F32).reshape(WIDE, 8, -1)
        for b in range(own.shape[2] // LANES):
            o = own[:, :, b * LANES : (b + 1) * LANES]
            h = halo[:, :, b * LANES : (b + 1) * LANES]
            z[b, 1 : WIDE + 1, 0:8, :] = h * above
            z[b, 1 : WIDE + 1, 8:16, :] = o[:, 0:8]
            z[b, 1 : WIDE + 1, 16:24, :] = o[:, 8:16] + h * edge
            z[b, 1 : WIDE + 1, 24:32, :] = h * below

    def fill_all(z, both):
        fill(z, both[: WIDE * 16], both[WIDE * 16 :])

    def column(z, b, flip, scale=None):
        acc = None
        for i in range(7):
            at = 5 + (6 - i if flip else i)
            k = kc_ref[i : i + 1, b * LANES : (b + 1) * LANES].reshape(1, 1, LANES)
            k = k if scale is None else k * scale
            t = z[b, 1 : WIDE + 1, at : at + 16, :] * k
            acc = t if acc is None else acc + t
        return acc

    def square(z, b, flip, scale=None):
        acc = None
        for i in range(3):
            at = 7 + (2 - i if flip else i)
            for j in range(3):
                w = 2 - j if flip else j
                k = ks_ref[i, j : j + 1, b * LANES : (b + 1) * LANES].reshape(1, 1, LANES)
                k = k if scale is None else k * scale
                t = z[b, w : w + WIDE, at : at + 16, :] * k
                acc = t if acc is None else acc + t
        return acc

    def pool(z, b):
        rows = (
            z[b, :, 7 : 7 + 16, :] + z[b, :, 8 : 8 + 16, :] + z[b, :, 9 : 9 + 16, :]
        )
        return (rows[0:WIDE] + rows[1 : WIDE + 1] + rows[2 : WIDE + 2]) * (1.0 / 9.0)

    def gather(parts):
        return jnp.concatenate([p.astype(BF16).reshape(WIDE * 16, LANES) for p in parts], axis=1)

    copies = []

    def put(stage, hbm, j, value):
        stage[j] = value.astype(BF16).reshape(WIDE, 16, C)[:, 0:ROWS, :]
        copy = pltpu.make_async_copy(
            stage.at[j], hbm.at[:, :, pl.ds(j * C, C)], sems.at[len(copies)]
        )
        copy.start()
        copies.append(copy)

    def flat(ref, lo, hi):
        v = ref[:, :, lo:hi]
        return v.reshape(-1, hi - lo)

    def rows_of(ref, lo, hi, halo_lo):
        return jnp.concatenate([flat(ref, lo, hi), flat(h_ref, halo_lo, halo_lo + hi - lo)], axis=0)

    ps = ps_ref[...]
    pc = pc_ref[...]
    fill_all(zs, dot_t(rows_of(g_s, 0, C, 2 * CIN), ps) * UNSCALE)
    fill_all(zc, dot_t(rows_of(g_s, C, 2 * C, 2 * CIN + C), pc) * UNSCALE)
    fill(zp, flat(g_s, 2 * C, 3 * C), flat(h_ref, 2 * CIN + 2 * C, 2 * CIN + 3 * C))

    half = C // 2
    older_rows = rows_of(xo_s, 0, CIN, 0)
    newer_rows = rows_of(xn_s, 0, CIN, CIN)
    newer_parts = []
    older_parts = []
    for n in range(2):
        both = dot(older_rows, wo_ref[:, n * half : (n + 1) * half]) * UNSCALE
        fill_all(zo.at[2 * n : 2 * n + 2], both)
        for b in (2 * n, 2 * n + 1):
            same = g_s[:, :, 3 * C + b * LANES : 3 * C + (b + 1) * LANES].astype(F32)
            newer_parts.append((square(zs, b, True) + same) * UNSCALE)
    mixed = []
    for n in range(2):
        both = dot(newer_rows, wn_ref[:, n * half : (n + 1) * half]) * UNSCALE
        fill_all(zn.at[2 * n : 2 * n + 2], both)
        mixed.append(both[: WIDE * 16].astype(BF16))
        for b in (2 * n, 2 * n + 1):
            older_parts.append((column(zc, b, True) + pool(zp, b)) * UNSCALE)
    put(cell_s, cell_hbm, 3, jnp.concatenate(mixed, axis=1))

    def grad_block(back, w_ref, x_s, stage, hbm, j):
        term = dot_t(back, w_ref[j * C : (j + 1) * C, :])
        positive = flat(x_s, j * C, (j + 1) * C).astype(F32) > 0
        put(stage, hbm, j, jnp.where(positive, term, 0.0))

    column_pre = []
    square_pre = []
    pooled = []
    back = gather(newer_parts)
    for j in range(4):
        grad_block(back, wn_ref, xn_s, ng_s, ng_hbm, j)
        column_pre.append(column(zo, j, False, UNSCALE))
        pooled.append(pool(zo, j))
    put(cell_s, cell_hbm, 2, gather(pooled))
    back = gather(older_parts)
    for j in range(4):
        grad_block(back, wo_ref, xo_s, og_s, og_hbm, j)
        square_pre.append(square(zn, j, False, UNSCALE))
    put(cell_s, cell_hbm, 1, dot(gather(column_pre), pc))
    put(cell_s, cell_hbm, 0, dot(gather(square_pre), ps))
    for copy in copies:
        copy.wait()


def placed(values, space):
    return [pltpu.with_memory_space_constraint(v, space) for v in values]


def run_halo(core, *operands):
    vmem = pl.BlockSpec(memory_space=pltpu.VMEM)
    hbm = pl.BlockSpec(memory_space=pltpu.HBM)
    padded = pltpu.VMEM((WIDE, 16, CIN), BF16)
    shards = sum(v.shape[0] for v in operands[3:])
    return pl.pallas_call(
        halo_kernel,
        out_shape=(padded,) * 3
        + (pltpu.VMEM((WIDE, 8, 3 * CIN), BF16), pltpu.VMEM((shards, C), BF16)),
        in_specs=[pl.BlockSpec(memory_space=pltpu.SMEM)] + [hbm] * 7,
        out_specs=(vmem,) * 5,
        scratch_shapes=[
            pltpu.VMEM((3, WIDE, ROWS, CIN), BF16),
            pltpu.SemaphoreType.DMA((3, PIECES)),
            pltpu.SemaphoreType.DMA((4,)),
        ],
        compiler_params=pltpu.CompilerParams(vmem_limit_bytes=16 * 1024 * 1024),
        name="halo",
    )(core, *placed(operands, pltpu.HBM))


def run_cell(core, *operands):
    vmem = pl.BlockSpec(memory_space=pltpu.VMEM)
    out = jax.ShapeDtypeStruct((WIDE, ROWS, CIN), BF16)
    field = pltpu.VMEM((BLOCKS, WIDE + 2, 32, LANES), F32)
    stage = pltpu.VMEM((4, WIDE, ROWS, C), BF16)
    return pl.pallas_call(
        cell_kernel,
        out_shape=(out, out, out),
        in_specs=[pl.BlockSpec(memory_space=pltpu.SMEM)] + [vmem] * 10,
        out_specs=(pl.BlockSpec(memory_space=pl.ANY),) * 3,
        scratch_shapes=[field] * 5 + [stage] * 3 + [pltpu.SemaphoreType.DMA((12,))],
        compiler_params=pltpu.CompilerParams(vmem_limit_bytes=24 * 1024 * 1024),
        name="cell",
    )(core, *placed(operands, pltpu.VMEM))


def local(
    older_output,
    newer_output,
    output_grad,
    older_weight,
    newer_weight,
    square_point,
    column_point,
    square_kernel,
    column_kernel,
):
    count = lax.axis_size("rows")
    core = lax.rem(lax.axis_index("rows"), 2)
    core = core.astype(jnp.int32).reshape(1)
    xo, xn, grad, rim, shard = run_halo(
        core,
        older_output.transpose(1, 0, 2),
        newer_output.transpose(1, 0, 2),
        output_grad.transpose(1, 0, 2),
        older_weight,
        newer_weight,
        square_point,
        column_point,
    )
    rim = lax.ppermute(rim, "rows", [(i, i ^ 1) for i in range(count)])
    shard = (shard * jnp.asarray(SCALE, BF16)).astype(jnp.float16)
    full = lax.all_gather(shard, "rows", axis=0, tiled=False)

    def part(lo, hi):
        piece = full[:, lo:hi].astype(BF16)
        return piece.reshape(-1, C)

    k = older_weight.shape[0]
    p = square_point.shape[0]
    cell, og, ng = run_cell(
        core,
        xo,
        xn,
        grad,
        rim,
        part(0, k),
        part(k, 2 * k),
        part(2 * k, 2 * k + p),
        part(2 * k + p, 2 * k + 2 * p),
        square_kernel,
        column_kernel,
    )
    return cell.transpose(1, 0, 2), og.transpose(1, 0, 2), ng.transpose(1, 0, 2)


def solution(mesh):
    rows = P(("dp", "rows"), None, None)
    in_specs = (rows, rows, rows) + (P("rows", None),) * 4 + (P(), P())
    return jax.shard_map(
        local, mesh=mesh, in_specs=in_specs, out_specs=(rows,) * 3, check_vma=False
    )
```

```python
import jax
import jax.numpy as jnp
from jax import lax
from jax.experimental import pallas as pl
from jax.experimental.pallas import tpu as pltpu
from jax.sharding import PartitionSpec as P

F32 = jnp.float32
BF16 = jnp.bfloat16
C = 512
CIN = 2048
WIDE = 12
ROWS = 15
LANES = 128
BLOCKS = C // LANES
PIECES = 4
SCALE = 2.0**17
UNSCALE = 1.0 / SCALE


def dot(a, b):
    return jnp.dot(a, b, preferred_element_type=F32)


def dot_t(a, b):
    return lax.dot_general(a, b, (((1,), (1,)), ((), ())), preferred_element_type=F32)


def halo_kernel(
    core_ref, xo_hbm, xn_hbm, g_hbm, wo_hbm, wn_hbm, ps_hbm, pc_hbm,
    xo_out, xn_out, g_out, h_out, w_out,
    raw, sems, weight_sems,
):
    first = core_ref[0] == 0
    turn = jnp.where(first, 1, 7)
    fields = ((xo_hbm, xo_out, True), (xn_hbm, xn_out, True), (g_hbm, g_out, False))
    copies = []
    for at, (src, _, _) in enumerate(fields):
        for q in range(PIECES):
            part = pl.ds(q * (WIDE // PIECES), WIDE // PIECES)
            copy = pltpu.make_async_copy(src.at[part], raw.at[at, part], sems.at[at, q])
            copy.start()
            copies.append(copy)
    row = 0
    loads = []
    for at, src in enumerate((wo_hbm, wn_hbm, ps_hbm, pc_hbm)):
        size = src.shape[0]
        copy = pltpu.make_async_copy(src, w_out.at[pl.ds(row, size)], weight_sems.at[at])
        copy.start()
        loads.append(copy)
        row += size
    for at, (_, dst, relu) in enumerate(fields):
        dst[:, 8:16, :] = jnp.zeros((WIDE, 8, CIN), BF16)
        for q in range(PIECES):
            copies[at * PIECES + q].wait()
        v = raw[at]
        dst[:, 0:ROWS, :] = jnp.maximum(v, 0) if relu else v
        sent = jnp.where(first, dst[:, 8:16, :].astype(F32), dst[:, 0:8, :].astype(F32))
        h_out[:, :, at * CIN : (at + 1) * CIN] = pltpu.roll(sent, turn, 1).astype(BF16)
    for copy in loads:
        copy.wait()


def cell_kernel(
    core_ref, xo_s, xn_s, g_s, h_ref, w_ref, ks_ref, kc_ref,
    cell_hbm, og_hbm, ng_hbm,
    zo, zn, zs, zc, zp, cell_s, og_s, ng_s, sems,
):
    slot = lax.broadcasted_iota(jnp.int32, (1, 8, LANES), 1)
    first = core_ref[0] == 0
    above = jnp.where((slot >= 5) & jnp.logical_not(first), 1.0, 0.0).astype(F32)
    below = jnp.where((slot < 2) & first, 1.0, 0.0).astype(F32)
    edge = jnp.where((slot == 7) & first, 1.0, 0.0).astype(F32)

    for z in (zo, zn, zs, zp):
        z[:, 0] = jnp.zeros((BLOCKS, 32, LANES), F32)
        z[:, WIDE + 1] = jnp.zeros((BLOCKS, 32, LANES), F32)

    def fill(z, own, halo):
        own = own.astype(BF16).astype(F32).reshape(WIDE, 16, -1)
        halo = halo.astype(BF16).astype(F32).reshape(WIDE, 8, -1)
        for b in range(own.shape[2] // LANES):
            o = own[:, :, b * LANES : (b + 1) * LANES]
            h = halo[:, :, b * LANES : (b + 1) * LANES]
            z[b, 1 : WIDE + 1, 0:8, :] = h * above
            z[b, 1 : WIDE + 1, 8:16, :] = o[:, 0:8]
            z[b, 1 : WIDE + 1, 16:24, :] = o[:, 8:16] + h * edge
            z[b, 1 : WIDE + 1, 24:32, :] = h * below

    def fill_all(z, both):
        fill(z, both[: WIDE * 16], both[WIDE * 16 :])

    def column(z, b, flip, scale=None):
        acc = None
        for i in range(7):
            at = 5 + (6 - i if flip else i)
            k = kc_ref[i : i + 1, b * LANES : (b + 1) * LANES].reshape(1, 1, LANES)
            k = k if scale is None else k * scale
            t = z[b, 1 : WIDE + 1, at : at + 16, :] * k
            acc = t if acc is None else acc + t
        return acc

    def square(z, b, flip, scale=None):
        acc = None
        for i in range(3):
            at = 7 + (2 - i if flip else i)
            for j in range(3):
                w = 2 - j if flip else j
                k = ks_ref[i, j : j + 1, b * LANES : (b + 1) * LANES].reshape(1, 1, LANES)
                k = k if scale is None else k * scale
                t = z[b, w : w + WIDE, at : at + 16, :] * k
                acc = t if acc is None else acc + t
        return acc

    def pool(z, b):
        rows = (
            z[b, :, 7 : 7 + 16, :] + z[b, :, 8 : 8 + 16, :] + z[b, :, 9 : 9 + 16, :]
        )
        return (rows[0:WIDE] + rows[1 : WIDE + 1] + rows[2 : WIDE + 2]) * (1.0 / 9.0)

    def gather(parts):
        return jnp.concatenate([p.astype(BF16).reshape(WIDE * 16, LANES) for p in parts], axis=1)

    copies = []

    def put(stage, hbm, j, value):
        stage[j] = value.astype(BF16).reshape(WIDE, 16, C)[:, 0:ROWS, :]
        copy = pltpu.make_async_copy(
            stage.at[j], hbm.at[:, :, pl.ds(j * C, C)], sems.at[len(copies)]
        )
        copy.start()
        copies.append(copy)

    def flat(ref, lo, hi):
        v = ref[:, :, lo:hi]
        return v.reshape(-1, hi - lo)

    def rows_of(ref, lo, hi, halo_lo):
        return jnp.concatenate([flat(ref, lo, hi), flat(h_ref, halo_lo, halo_lo + hi - lo)], axis=0)

    shards = w_ref.shape[0]
    deep = CIN // shards
    flatter = C // shards

    def weight(at, lo, hi, first_row=0, last_row=CIN):
        pieces = range(first_row // deep, last_row // deep)
        return jnp.concatenate([w_ref[s, at : at + deep, lo:hi] for s in pieces], axis=0)

    def point(at):
        return jnp.concatenate([w_ref[s, at : at + flatter, :] for s in range(shards)], axis=0)

    ps = point(2 * deep)
    pc = point(2 * deep + flatter)
    fill_all(zs, dot_t(rows_of(g_s, 0, C, 2 * CIN), ps) * UNSCALE)
    fill_all(zc, dot_t(rows_of(g_s, C, 2 * C, 2 * CIN + C), pc) * UNSCALE)
    fill(zp, flat(g_s, 2 * C, 3 * C), flat(h_ref, 2 * CIN + 2 * C, 2 * CIN + 3 * C))

    half = C // 2
    older_rows = rows_of(xo_s, 0, CIN, 0)
    newer_rows = rows_of(xn_s, 0, CIN, CIN)
    newer_parts = []
    older_parts = []
    column_pre = []
    square_pre = []
    pooled = []
    mixed = []

    def newer_part(b):
        same = g_s[:, :, 3 * C + b * LANES : 3 * C + (b + 1) * LANES].astype(F32)
        newer_parts.append((square(zs, b, True) + same) * UNSCALE)

    def older_part(b):
        older_parts.append((column(zc, b, True) + pool(zp, b)) * UNSCALE)

    def older_half(n):
        both = dot(older_rows, weight(0, n * half, (n + 1) * half)) * UNSCALE
        fill_all(zo.at[2 * n : 2 * n + 2], both)

    def newer_half(n):
        both = dot(newer_rows, weight(deep, n * half, (n + 1) * half)) * UNSCALE
        fill_all(zn.at[2 * n : 2 * n + 2], both)
        mixed.append(both[: WIDE * 16].astype(BF16))

    def forward_older(b):
        column_pre.append(column(zo, b, False, UNSCALE))
        pooled.append(pool(zo, b))

    def grad_block(back, at, x_s, stage, hbm, j):
        term = dot_t(back, weight(at, 0, C, j * C, (j + 1) * C)).astype(BF16)
        positive = flat(x_s, j * C, (j + 1) * C) > 0
        put(stage, hbm, j, jnp.where(positive, term, jnp.zeros_like(term)))

    for n in range(2):
        older_half(n)
        newer_part(2 * n)
        newer_part(2 * n + 1)
    for n in range(2):
        newer_half(n)
        older_part(2 * n)
        older_part(2 * n + 1)
    put(cell_s, cell_hbm, 3, jnp.concatenate(mixed, axis=1))
    back = gather(newer_parts)
    for j in range(4):
        grad_block(back, deep, xn_s, ng_s, ng_hbm, j)
        forward_older(j)
    put(cell_s, cell_hbm, 2, gather(pooled))
    back = gather(older_parts)
    for j in range(4):
        grad_block(back, 0, xo_s, og_s, og_hbm, j)
        square_pre.append(square(zn, j, False, UNSCALE))
    put(cell_s, cell_hbm, 1, dot(gather(column_pre), pc))
    put(cell_s, cell_hbm, 0, dot(gather(square_pre), ps))
    for copy in copies:
        copy.wait()


def placed(values, space):
    return [pltpu.with_memory_space_constraint(v, space) for v in values]


def run_halo(core, *operands):
    vmem = pl.BlockSpec(memory_space=pltpu.VMEM)
    hbm = pl.BlockSpec(memory_space=pltpu.HBM)
    padded = pltpu.VMEM((WIDE, 16, CIN), BF16)
    shards = sum(v.shape[0] for v in operands[3:])
    return pl.pallas_call(
        halo_kernel,
        out_shape=(padded,) * 3
        + (pltpu.VMEM((WIDE, 8, 3 * CIN), BF16), pltpu.VMEM((shards, C), BF16)),
        in_specs=[pl.BlockSpec(memory_space=pltpu.SMEM)] + [hbm] * 7,
        out_specs=(vmem,) * 5,
        scratch_shapes=[
            pltpu.VMEM((3, WIDE, ROWS, CIN), BF16),
            pltpu.SemaphoreType.DMA((3, PIECES)),
            pltpu.SemaphoreType.DMA((4,)),
        ],
        compiler_params=pltpu.CompilerParams(vmem_limit_bytes=16 * 1024 * 1024),
        name="halo",
    )(core, *placed(operands, pltpu.HBM))


def run_cell(core, *operands):
    vmem = pl.BlockSpec(memory_space=pltpu.VMEM)
    out = jax.ShapeDtypeStruct((WIDE, ROWS, CIN), BF16)
    field = pltpu.VMEM((BLOCKS, WIDE + 2, 32, LANES), F32)
    stage = pltpu.VMEM((4, WIDE, ROWS, C), BF16)
    return pl.pallas_call(
        cell_kernel,
        out_shape=(out, out, out),
        in_specs=[pl.BlockSpec(memory_space=pltpu.SMEM)] + [vmem] * 7,
        out_specs=(pl.BlockSpec(memory_space=pl.ANY),) * 3,
        scratch_shapes=[field] * 5 + [stage] * 3 + [pltpu.SemaphoreType.DMA((12,))],
        compiler_params=pltpu.CompilerParams(vmem_limit_bytes=24 * 1024 * 1024),
        name="cell",
    )(core, *placed(operands, pltpu.VMEM))


def local(
    older_output,
    newer_output,
    output_grad,
    older_weight,
    newer_weight,
    square_point,
    column_point,
    square_kernel,
    column_kernel,
):
    count = lax.axis_size("rows")
    core = lax.rem(lax.axis_index("rows"), 2)
    core = core.astype(jnp.int32).reshape(1)
    xo, xn, grad, rim, shard = run_halo(
        core,
        older_output.transpose(1, 0, 2),
        newer_output.transpose(1, 0, 2),
        output_grad.transpose(1, 0, 2),
        older_weight,
        newer_weight,
        square_point,
        column_point,
    )
    rim = lax.ppermute(rim, "rows", [(i, i ^ 1) for i in range(count)])
    shard = (shard * jnp.asarray(SCALE, BF16)).astype(jnp.float16)
    full = lax.all_gather(shard, "rows", axis=0, tiled=False).astype(BF16)

    cell, og, ng = run_cell(
        core,
        xo,
        xn,
        grad,
        rim,
        full,
        square_kernel,
        column_kernel,
    )
    return cell.transpose(1, 0, 2), og.transpose(1, 0, 2), ng.transpose(1, 0, 2)


def solution(mesh):
    rows = P(("dp", "rows"), None, None)
    in_specs = (rows, rows, rows) + (P("rows", None),) * 4 + (P(), P())
    return jax.shard_map(
        local, mesh=mesh, in_specs=in_specs, out_specs=(rows,) * 3, check_vma=False
    )
```

```python
import jax
import jax.numpy as jnp
from jax import lax
from jax.experimental import pallas as pl
from jax.experimental.pallas import tpu as pltpu
from jax.sharding import PartitionSpec as P

F32 = jnp.float32
BF16 = jnp.bfloat16
C = 512
CIN = 2048
WIDE = 12
ROWS = 15
LANES = 128
BLOCKS = C // LANES
PIECES = 1
OWN = WIDE * 16
FAR = WIDE * 8
SCALE = 2.0**17
UNSCALE = 1.0 / SCALE


def dot(a, b):
    return jnp.dot(a, b, preferred_element_type=F32)


def dot_t(a, b):
    return lax.dot_general(a, b, (((1,), (1,)), ((), ())), preferred_element_type=F32)


def halo_kernel(
    core_ref, xo_hbm, xn_hbm, g_hbm, wo_hbm, wn_hbm, ps_hbm, pc_hbm,
    xo_out, xn_out, g_out, h_out, w_out,
    raw, sems, weight_sems,
):
    first = core_ref[0] == 0
    turn = jnp.where(first, 1, 7)

    def far(rows):
        return rows.reshape(FAR, rows.shape[2]).astype(BF16)

    def near(rows):
        last = lax.broadcasted_iota(jnp.int32, rows.shape, 1) == 7
        both = jnp.concatenate([jnp.zeros_like(rows), jnp.where(last, rows, 0.0)], axis=1)
        return both.reshape(OWN, rows.shape[2]).astype(BF16)

    fields = ((xo_hbm, xo_out, True), (xn_hbm, xn_out, True), (g_hbm, g_out, False))
    copies = []
    for at, (src, _, _) in enumerate(fields):
        for q in range(PIECES):
            part = pl.ds(q * (WIDE // PIECES), WIDE // PIECES)
            copy = pltpu.make_async_copy(src.at[part], raw.at[at, part], sems.at[at, q])
            copy.start()
            copies.append(copy)
    row = 0
    loads = []
    for at, src in enumerate((wo_hbm, wn_hbm, ps_hbm, pc_hbm)):
        size = src.shape[0]
        copy = pltpu.make_async_copy(src, w_out.at[pl.ds(row, size)], weight_sems.at[at])
        copy.start()
        loads.append(copy)
        row += size
    for at, (_, dst, relu) in enumerate(fields):
        dst[:, 8:16, :] = jnp.zeros((WIDE, 8, CIN), BF16)
        for q in range(PIECES):
            copies[at * PIECES + q].wait()
        v = raw[at]
        dst[:, 0:ROWS, :] = jnp.maximum(v, 0) if relu else v
        width = 3 * C if at == 2 else CIN
        sent = jnp.where(
            first, dst[:, 8:16, :width].astype(F32), dst[:, 0:8, :width].astype(F32)
        )
        sent = pltpu.roll(sent, turn, 1)
        if at == 0:
            h_out[0:FAR, :] = far(sent)
        elif at == 1:
            h_out[FAR : FAR + OWN, :] = near(sent)
        else:
            h_out[FAR + OWN :, 0:C] = near(sent[:, :, 0:C])
            h_out[FAR + OWN : FAR + OWN + FAR, C : 2 * C] = far(sent[:, :, C : 2 * C])
            h_out[FAR + OWN :, 2 * C : 3 * C] = near(sent[:, :, 2 * C : 3 * C])
    for copy in loads:
        copy.wait()


def cell_kernel(
    core_ref, xo_s, xn_s, g_s, h_ref, w_ref, ks_ref, kc_ref,
    cell_hbm, og_hbm, ng_hbm,
    zo, zn, zs, zc, zp, cell_s, og_s, ng_s, sems,
):
    slot = lax.broadcasted_iota(jnp.int32, (1, 8, LANES), 1)
    first = core_ref[0] == 0
    above = jnp.where((slot >= 5) & jnp.logical_not(first), 1.0, 0.0).astype(F32)
    below = jnp.where((slot < 2) & first, 1.0, 0.0).astype(F32)
    edge = jnp.where((slot == 7) & first, 1.0, 0.0).astype(F32)
    before = jnp.where((slot == 7) & jnp.logical_not(first), 1.0, 0.0).astype(F32)
    after = jnp.where((slot < 7) | first, 1.0, 0.0).astype(F32)

    for z in (zo, zn, zs, zp):
        z[:, 0] = jnp.zeros((BLOCKS, 32, LANES), F32)
        z[:, WIDE + 1] = jnp.zeros((BLOCKS, 32, LANES), F32)

    def fill(z, own, halo):
        own = own.astype(BF16).astype(F32).reshape(WIDE, 16, -1)
        halo = halo.astype(BF16).astype(F32).reshape(WIDE, 8, -1)
        for b in range(own.shape[2] // LANES):
            o = own[:, :, b * LANES : (b + 1) * LANES]
            h = halo[:, :, b * LANES : (b + 1) * LANES]
            z[b, 1 : WIDE + 1, 0:8, :] = h * above
            z[b, 1 : WIDE + 1, 8:16, :] = o[:, 0:8]
            z[b, 1 : WIDE + 1, 16:24, :] = o[:, 8:16] + h * edge
            z[b, 1 : WIDE + 1, 24:32, :] = h * below

    def fill_all(z, both):
        fill(z, both[:OWN], both[OWN:])

    def fill_near(z, own):
        own = own.astype(BF16).astype(F32).reshape(WIDE, 16, -1)
        for b in range(own.shape[2] // LANES):
            o = own[:, :, b * LANES : (b + 1) * LANES]
            z[b, 1 : WIDE + 1, 0:8, :] = o[:, 8:16] * before
            z[b, 1 : WIDE + 1, 8:16, :] = o[:, 0:8]
            z[b, 1 : WIDE + 1, 16:24, :] = o[:, 8:16] * after
            z[b, 1 : WIDE + 1, 24:32, :] = jnp.zeros((WIDE, 8, LANES), F32)

    def column(z, b, flip, scale=None):
        acc = None
        for i in range(7):
            at = 5 + (6 - i if flip else i)
            k = kc_ref[i : i + 1, b * LANES : (b + 1) * LANES].reshape(1, 1, LANES)
            k = k if scale is None else k * scale
            t = z[b, 1 : WIDE + 1, at : at + 16, :] * k
            acc = t if acc is None else acc + t
        return acc

    def square(z, b, flip, scale=None):
        acc = None
        for i in range(3):
            at = 7 + (2 - i if flip else i)
            for j in range(3):
                w = 2 - j if flip else j
                k = ks_ref[i, j : j + 1, b * LANES : (b + 1) * LANES].reshape(1, 1, LANES)
                k = k if scale is None else k * scale
                t = z[b, w : w + WIDE, at : at + 16, :] * k
                acc = t if acc is None else acc + t
        return acc

    def pool(z, b):
        rows = (
            z[b, :, 7 : 7 + 16, :] + z[b, :, 8 : 8 + 16, :] + z[b, :, 9 : 9 + 16, :]
        )
        return (rows[0:WIDE] + rows[1 : WIDE + 1] + rows[2 : WIDE + 2]) * (1.0 / 9.0)

    def gather(parts):
        return jnp.concatenate([p.astype(BF16).reshape(WIDE * 16, LANES) for p in parts], axis=1)

    copies = []

    def put(stage, hbm, j, value):
        stage[j] = value.astype(BF16).reshape(WIDE, 16, C)[:, 0:ROWS, :]
        copy = pltpu.make_async_copy(
            stage.at[j], hbm.at[:, :, pl.ds(j * C, C)], sems.at[len(copies)]
        )
        copy.start()
        copies.append(copy)

    def flat(ref, lo, hi):
        v = ref[:, :, lo:hi]
        return v.reshape(-1, hi - lo)

    def with_far(own, rows, lo):
        return jnp.concatenate([own, h_ref[rows : rows + FAR, lo : lo + own.shape[1]]], axis=0)

    def with_near(own, rows, lo):
        return own + h_ref[rows : rows + OWN, lo : lo + own.shape[1]]

    shards = w_ref.shape[0]
    deep = CIN // shards
    flatter = C // shards

    def weight(at, lo, hi, first_row=0, last_row=CIN):
        pieces = range(first_row // deep, last_row // deep)
        return jnp.concatenate([w_ref[s, at : at + deep, lo:hi] for s in pieces], axis=0)

    def point(at):
        return jnp.concatenate([w_ref[s, at : at + flatter, :] for s in range(shards)], axis=0)

    ps = point(2 * deep)
    pc = point(2 * deep + flatter)
    base = FAR + OWN
    fill_near(zs, dot_t(with_near(flat(g_s, 0, C), base, 0), ps) * UNSCALE)
    fill_all(zc, dot_t(with_far(flat(g_s, C, 2 * C), base, C), pc) * UNSCALE)
    fill_near(zp, with_near(flat(g_s, 2 * C, 3 * C), base, 2 * C))

    half = C // 2
    older_rows = with_far(flat(xo_s, 0, CIN), 0, 0)
    newer_rows = with_near(flat(xn_s, 0, CIN), FAR, 0)
    newer_parts = []
    older_parts = []
    column_pre = []
    square_pre = []
    pooled = []
    mixed = []

    def newer_part(b):
        same = g_s[:, :, 3 * C + b * LANES : 3 * C + (b + 1) * LANES].astype(F32)
        newer_parts.append((square(zs, b, True) + same) * UNSCALE)

    def older_part(b):
        older_parts.append((column(zc, b, True) + pool(zp, b)) * UNSCALE)

    def older_half(n):
        both = dot(older_rows, weight(0, n * half, (n + 1) * half)) * UNSCALE
        fill_all(zo.at[2 * n : 2 * n + 2], both)

    def newer_half(n):
        both = dot(newer_rows, weight(deep, n * half, (n + 1) * half)) * UNSCALE
        fill_near(zn.at[2 * n : 2 * n + 2], both)
        mixed.append(both.astype(BF16))

    def forward_older(b):
        column_pre.append(column(zo, b, False, UNSCALE))
        pooled.append(pool(zo, b))

    def grad_block(back, at, x_s, stage, hbm, j):
        term = dot_t(back, weight(at, 0, C, j * C, (j + 1) * C)).astype(BF16)
        positive = flat(x_s, j * C, (j + 1) * C) > 0
        put(stage, hbm, j, jnp.where(positive, term, jnp.zeros_like(term)))

    for n in range(2):
        older_half(n)
        newer_part(2 * n)
        newer_part(2 * n + 1)
    for n in range(2):
        newer_half(n)
        older_part(2 * n)
        older_part(2 * n + 1)
    put(cell_s, cell_hbm, 3, jnp.concatenate(mixed, axis=1))
    back = gather(newer_parts)
    for j in range(4):
        grad_block(back, deep, xn_s, ng_s, ng_hbm, j)
        forward_older(j)
    put(cell_s, cell_hbm, 2, gather(pooled))
    back = gather(older_parts)
    for j in range(4):
        grad_block(back, 0, xo_s, og_s, og_hbm, j)
        square_pre.append(square(zn, j, False, UNSCALE))
    put(cell_s, cell_hbm, 1, dot(gather(column_pre), pc))
    put(cell_s, cell_hbm, 0, dot(gather(square_pre), ps))
    for copy in copies:
        copy.wait()


def placed(values, space):
    return [pltpu.with_memory_space_constraint(v, space) for v in values]


def run_halo(core, *operands):
    vmem = pl.BlockSpec(memory_space=pltpu.VMEM)
    hbm = pl.BlockSpec(memory_space=pltpu.HBM)
    padded = pltpu.VMEM((WIDE, 16, CIN), BF16)
    shards = sum(v.shape[0] for v in operands[3:])
    return pl.pallas_call(
        halo_kernel,
        out_shape=(padded,) * 3
        + (pltpu.VMEM((FAR + 2 * OWN, CIN), BF16), pltpu.VMEM((shards, C), BF16)),
        in_specs=[pl.BlockSpec(memory_space=pltpu.SMEM)] + [hbm] * 7,
        out_specs=(vmem,) * 5,
        scratch_shapes=[
            pltpu.VMEM((3, WIDE, ROWS, CIN), BF16),
            pltpu.SemaphoreType.DMA((3, PIECES)),
            pltpu.SemaphoreType.DMA((4,)),
        ],
        compiler_params=pltpu.CompilerParams(vmem_limit_bytes=16 * 1024 * 1024),
        name="halo",
    )(core, *placed(operands, pltpu.HBM))


def run_cell(core, *operands):
    vmem = pl.BlockSpec(memory_space=pltpu.VMEM)
    out = jax.ShapeDtypeStruct((WIDE, ROWS, CIN), BF16)
    field = pltpu.VMEM((BLOCKS, WIDE + 2, 32, LANES), F32)
    stage = pltpu.VMEM((4, WIDE, ROWS, C), BF16)
    return pl.pallas_call(
        cell_kernel,
        out_shape=(out, out, out),
        in_specs=[pl.BlockSpec(memory_space=pltpu.SMEM)] + [vmem] * 7,
        out_specs=(pl.BlockSpec(memory_space=pl.ANY),) * 3,
        scratch_shapes=[field] * 5 + [stage] * 3 + [pltpu.SemaphoreType.DMA((12,))],
        compiler_params=pltpu.CompilerParams(vmem_limit_bytes=24 * 1024 * 1024),
        name="cell",
    )(core, *placed(operands, pltpu.VMEM))


def local(
    older_output,
    newer_output,
    output_grad,
    older_weight,
    newer_weight,
    square_point,
    column_point,
    square_kernel,
    column_kernel,
):
    count = lax.axis_size("rows")
    core = lax.rem(lax.axis_index("rows"), 2)
    core = core.astype(jnp.int32).reshape(1)
    xo, xn, grad, rim, shard = run_halo(
        core,
        older_output.transpose(1, 0, 2),
        newer_output.transpose(1, 0, 2),
        output_grad.transpose(1, 0, 2),
        older_weight,
        newer_weight,
        square_point,
        column_point,
    )
    rim = lax.ppermute(rim, "rows", [(i, i ^ 1) for i in range(count)])
    shard = (shard * jnp.asarray(SCALE, BF16)).astype(jnp.float16)
    full = lax.all_gather(shard, "rows", axis=0, tiled=False).astype(BF16)

    cell, og, ng = run_cell(
        core,
        xo,
        xn,
        grad,
        rim,
        full,
        square_kernel,
        column_kernel,
    )
    return cell.transpose(1, 0, 2), og.transpose(1, 0, 2), ng.transpose(1, 0, 2)


def solution(mesh):
    rows = P(("dp", "rows"), None, None)
    in_specs = (rows, rows, rows) + (P("rows", None),) * 4 + (P(), P())
    return jax.shard_map(
        local, mesh=mesh, in_specs=in_specs, out_specs=(rows,) * 3, check_vma=False
    )
```

```python
import jax
import jax.numpy as jnp
from jax import lax
from jax.experimental import pallas as pl
from jax.experimental.pallas import tpu as pltpu
from jax.sharding import PartitionSpec as P

F32 = jnp.float32
BF16 = jnp.bfloat16
C = 512
CIN = 2048
WIDE = 12
ROWS = 15
LANES = 128
BLOCKS = C // LANES
PIECES = 1
OWN = WIDE * 16
FAR = WIDE * 8
SCALE = 2.0**17
UNSCALE = 1.0 / SCALE


def dot(a, b):
    return jnp.dot(a, b, preferred_element_type=F32)


def dot_t(a, b):
    return lax.dot_general(a, b, (((1,), (1,)), ((), ())), preferred_element_type=F32)


def halo_kernel(
    core_ref, xo_hbm, xn_hbm, g_hbm, wo_hbm, wn_hbm, ps_hbm, pc_hbm,
    xo_out, xn_out, g_out, h_out, w_out,
    raw, sems, weight_sems,
):
    first = core_ref[0] == 0
    turn = jnp.where(first, 1, 7)

    def far(rows):
        return rows.reshape(FAR, rows.shape[2]).astype(BF16)

    def near(rows):
        last = lax.broadcasted_iota(jnp.int32, rows.shape, 1) == 7
        both = jnp.concatenate([jnp.zeros_like(rows), jnp.where(last, rows, 0.0)], axis=1)
        return both.reshape(OWN, rows.shape[2]).astype(BF16)

    fields = ((xo_hbm, xo_out, True), (xn_hbm, xn_out, True), (g_hbm, g_out, False))
    copies = []
    for at, (src, _, _) in enumerate(fields):
        for q in range(PIECES):
            part = pl.ds(q * (WIDE // PIECES), WIDE // PIECES)
            copy = pltpu.make_async_copy(src.at[part], raw.at[at, part], sems.at[at, q])
            copy.start()
            copies.append(copy)
    row = 0
    loads = []
    for at, src in enumerate((wo_hbm, wn_hbm, ps_hbm, pc_hbm)):
        size = src.shape[0]
        copy = pltpu.make_async_copy(src, w_out.at[pl.ds(row, size)], weight_sems.at[at])
        copy.start()
        loads.append(copy)
        row += size
    for at, (_, dst, relu) in enumerate(fields):
        dst[:, 8:16, :] = jnp.zeros((WIDE, 8, CIN), BF16)
        for q in range(PIECES):
            copies[at * PIECES + q].wait()
        v = raw[at]
        dst[:, 0:ROWS, :] = jnp.maximum(v, 0) if relu else v
        width = 3 * C if at == 2 else CIN
        sent = jnp.where(
            first, dst[:, 8:16, :width].astype(F32), dst[:, 0:8, :width].astype(F32)
        )
        sent = pltpu.roll(sent, turn, 1)
        if at == 0:
            h_out[0:FAR, :] = far(sent)
        elif at == 1:
            h_out[FAR : FAR + OWN, :] = near(sent)
        else:
            h_out[FAR + OWN :, 0:C] = near(sent[:, :, 0:C])
            h_out[FAR + OWN : FAR + OWN + FAR, C : 2 * C] = far(sent[:, :, C : 2 * C])
            h_out[FAR + OWN :, 2 * C : 3 * C] = near(sent[:, :, 2 * C : 3 * C])
    for copy in loads:
        copy.wait()


def cell_kernel(
    core_ref, xo_s, xn_s, g_s, h_ref, w_ref, ks_ref, kc_ref,
    cell_hbm, og_hbm, ng_hbm,
    zo, zn, zs, zc, zp, cell_s, og_s, ng_s, sems,
):
    slot = lax.broadcasted_iota(jnp.int32, (1, 8, LANES), 1)
    first = core_ref[0] == 0
    above = jnp.where((slot >= 5) & jnp.logical_not(first), 1.0, 0.0).astype(F32)
    below = jnp.where((slot < 2) & first, 1.0, 0.0).astype(F32)
    edge = jnp.where((slot == 7) & first, 1.0, 0.0).astype(F32)
    before = jnp.where((slot == 7) & jnp.logical_not(first), 1.0, 0.0).astype(F32)
    after = jnp.where((slot < 7) | first, 1.0, 0.0).astype(F32)

    for z in (zo, zn, zs, zp):
        z[:, 0] = jnp.zeros((BLOCKS, 32, LANES), F32)
        z[:, WIDE + 1] = jnp.zeros((BLOCKS, 32, LANES), F32)

    def fill(z, own, halo):
        own = own.astype(BF16).astype(F32).reshape(WIDE, 16, -1)
        halo = halo.astype(BF16).astype(F32).reshape(WIDE, 8, -1)
        for b in range(own.shape[2] // LANES):
            o = own[:, :, b * LANES : (b + 1) * LANES]
            h = halo[:, :, b * LANES : (b + 1) * LANES]
            z[b, 1 : WIDE + 1, 0:8, :] = h * above
            z[b, 1 : WIDE + 1, 8:16, :] = o[:, 0:8]
            z[b, 1 : WIDE + 1, 16:24, :] = o[:, 8:16] + h * edge
            z[b, 1 : WIDE + 1, 24:32, :] = h * below

    def fill_all(z, both):
        fill(z, both[:OWN], both[OWN:])

    def fill_near(z, own):
        own = own.astype(BF16).astype(F32).reshape(WIDE, 16, -1)
        for b in range(own.shape[2] // LANES):
            o = own[:, :, b * LANES : (b + 1) * LANES]
            z[b, 1 : WIDE + 1, 0:8, :] = o[:, 8:16] * before
            z[b, 1 : WIDE + 1, 8:16, :] = o[:, 0:8]
            z[b, 1 : WIDE + 1, 16:24, :] = o[:, 8:16] * after
            z[b, 1 : WIDE + 1, 24:32, :] = jnp.zeros((WIDE, 8, LANES), F32)

    def column(z, b, flip, scale=None):
        acc = None
        for i in range(7):
            at = 5 + (6 - i if flip else i)
            k = kc_ref[i : i + 1, b * LANES : (b + 1) * LANES].reshape(1, 1, LANES)
            k = k if scale is None else k * scale
            t = z[b, 1 : WIDE + 1, at : at + 16, :] * k
            acc = t if acc is None else acc + t
        return acc

    def square(z, b, flip, scale=None):
        acc = None
        for i in range(3):
            at = 7 + (2 - i if flip else i)
            for j in range(3):
                w = 2 - j if flip else j
                k = ks_ref[i, j : j + 1, b * LANES : (b + 1) * LANES].reshape(1, 1, LANES)
                k = k if scale is None else k * scale
                t = z[b, w : w + WIDE, at : at + 16, :] * k
                acc = t if acc is None else acc + t
        return acc

    def pool(z, b):
        rows = (
            z[b, :, 7 : 7 + 16, :] + z[b, :, 8 : 8 + 16, :] + z[b, :, 9 : 9 + 16, :]
        )
        return (rows[0:WIDE] + rows[1 : WIDE + 1] + rows[2 : WIDE + 2]) * (1.0 / 9.0)

    def gather(parts):
        return jnp.concatenate([p.astype(BF16).reshape(WIDE * 16, LANES) for p in parts], axis=1)

    copies = []

    def put(stage, hbm, j, value):
        stage[j] = value.astype(BF16).reshape(WIDE, 16, C)[:, 0:ROWS, :]
        copy = pltpu.make_async_copy(
            stage.at[j], hbm.at[:, :, pl.ds(j * C, C)], sems.at[len(copies)]
        )
        copy.start()
        copies.append(copy)

    def flat(ref, lo, hi):
        v = ref[:, :, lo:hi]
        return v.reshape(-1, hi - lo)

    def with_far(own, rows, lo):
        return jnp.concatenate([own, h_ref[rows : rows + FAR, lo : lo + own.shape[1]]], axis=0)

    def with_near(own, rows, lo):
        return own + h_ref[rows : rows + OWN, lo : lo + own.shape[1]]

    shards = w_ref.shape[0]
    deep = CIN // shards
    flatter = C // shards

    def weight(at, lo, hi, first_row=0, last_row=CIN):
        pieces = range(first_row // deep, last_row // deep)
        return jnp.concatenate([w_ref[s, at : at + deep, lo:hi] for s in pieces], axis=0)

    def point(at):
        return jnp.concatenate([w_ref[s, at : at + flatter, :] for s in range(shards)], axis=0)

    ps = point(2 * deep)
    pc = point(2 * deep + flatter)
    base = FAR + OWN
    fill_near(zs, dot_t(with_near(flat(g_s, 0, C), base, 0), ps) * UNSCALE)
    fill_all(zc, dot_t(with_far(flat(g_s, C, 2 * C), base, C), pc) * UNSCALE)
    fill_near(zp, with_near(flat(g_s, 2 * C, 3 * C), base, 2 * C))

    half = C // 2
    older_rows = with_far(flat(xo_s, 0, CIN), 0, 0)
    newer_rows = with_near(flat(xn_s, 0, CIN), FAR, 0)
    newer_parts = []
    older_parts = []
    column_pre = []
    square_pre = []
    pooled = []
    mixed = []

    def newer_part(b):
        same = g_s[:, :, 3 * C + b * LANES : 3 * C + (b + 1) * LANES].astype(F32)
        newer_parts.append((square(zs, b, True) + same) * UNSCALE)

    def older_part(b):
        older_parts.append((column(zc, b, True) + pool(zp, b)) * UNSCALE)

    def older_half(n):
        both = dot(older_rows, weight(0, n * half, (n + 1) * half)) * UNSCALE
        fill_all(zo.at[2 * n : 2 * n + 2], both)

    def newer_half(n):
        both = dot(newer_rows, weight(deep, n * half, (n + 1) * half)) * UNSCALE
        fill_near(zn.at[2 * n : 2 * n + 2], both)
        mixed.append(both.astype(BF16))

    def forward_older(b):
        column_pre.append(column(zo, b, False, UNSCALE))
        pooled.append(pool(zo, b))

    def grad_block(back, at, x_s, stage, hbm, j):
        term = dot_t(weight(at, 0, C, j * C, (j + 1) * C), back).astype(BF16).T
        positive = flat(x_s, j * C, (j + 1) * C) > 0
        put(stage, hbm, j, jnp.where(positive, term, jnp.zeros_like(term)))

    for n in range(2):
        older_half(n)
        newer_part(2 * n)
        newer_part(2 * n + 1)
    for n in range(2):
        newer_half(n)
        older_part(2 * n)
        older_part(2 * n + 1)
    put(cell_s, cell_hbm, 3, jnp.concatenate(mixed, axis=1))
    back = gather(newer_parts)
    for j in range(4):
        grad_block(back, deep, xn_s, ng_s, ng_hbm, j)
        forward_older(j)
    put(cell_s, cell_hbm, 2, gather(pooled))
    back = gather(older_parts)
    for j in range(4):
        grad_block(back, 0, xo_s, og_s, og_hbm, j)
        square_pre.append(square(zn, j, False, UNSCALE))
    put(cell_s, cell_hbm, 1, dot(gather(column_pre), pc))
    pre = gather(square_pre)
    for n in range(2):
        lanes = pl.ds(n * half, half)
        value = dot(pre, ps[:, n * half : (n + 1) * half]).astype(BF16)
        cell_s[0, :, :, lanes] = value.reshape(WIDE, 16, half)[:, 0:ROWS, :]
        copy = pltpu.make_async_copy(
            cell_s.at[0, :, :, lanes], cell_hbm.at[:, :, lanes], sems.at[len(copies)]
        )
        copy.start()
        copies.append(copy)
    for copy in copies:
        copy.wait()


def placed(values, space):
    return [pltpu.with_memory_space_constraint(v, space) for v in values]


def run_halo(core, *operands):
    vmem = pl.BlockSpec(memory_space=pltpu.VMEM)
    hbm = pl.BlockSpec(memory_space=pltpu.HBM)
    padded = pltpu.VMEM((WIDE, 16, CIN), BF16)
    shards = sum(v.shape[0] for v in operands[3:])
    return pl.pallas_call(
        halo_kernel,
        out_shape=(padded,) * 3
        + (pltpu.VMEM((FAR + 2 * OWN, CIN), BF16), pltpu.VMEM((shards, C), BF16)),
        in_specs=[pl.BlockSpec(memory_space=pltpu.SMEM)] + [hbm] * 7,
        out_specs=(vmem,) * 5,
        scratch_shapes=[
            pltpu.VMEM((3, WIDE, ROWS, CIN), BF16),
            pltpu.SemaphoreType.DMA((3, PIECES)),
            pltpu.SemaphoreType.DMA((4,)),
        ],
        compiler_params=pltpu.CompilerParams(vmem_limit_bytes=16 * 1024 * 1024),
        name="halo",
    )(core, *placed(operands, pltpu.HBM))


def run_cell(core, *operands):
    vmem = pl.BlockSpec(memory_space=pltpu.VMEM)
    out = jax.ShapeDtypeStruct((WIDE, ROWS, CIN), BF16)
    field = pltpu.VMEM((BLOCKS, WIDE + 2, 32, LANES), F32)
    stage = pltpu.VMEM((4, WIDE, ROWS, C), BF16)
    return pl.pallas_call(
        cell_kernel,
        out_shape=(out, out, out),
        in_specs=[pl.BlockSpec(memory_space=pltpu.SMEM)] + [vmem] * 7,
        out_specs=(pl.BlockSpec(memory_space=pl.ANY),) * 3,
        scratch_shapes=[field] * 5 + [stage] * 3 + [pltpu.SemaphoreType.DMA((13,))],
        compiler_params=pltpu.CompilerParams(vmem_limit_bytes=24 * 1024 * 1024),
        name="cell",
    )(core, *placed(operands, pltpu.VMEM))


def local(
    older_output,
    newer_output,
    output_grad,
    older_weight,
    newer_weight,
    square_point,
    column_point,
    square_kernel,
    column_kernel,
):
    count = lax.axis_size("rows")
    core = lax.rem(lax.axis_index("rows"), 2)
    core = core.astype(jnp.int32).reshape(1)
    xo, xn, grad, rim, shard = run_halo(
        core,
        older_output.transpose(1, 0, 2),
        newer_output.transpose(1, 0, 2),
        output_grad.transpose(1, 0, 2),
        older_weight,
        newer_weight,
        square_point,
        column_point,
    )
    rim = lax.ppermute(rim, "rows", [(i, i ^ 1) for i in range(count)])
    shard = (shard * jnp.asarray(SCALE, BF16)).astype(jnp.float16)
    full = lax.all_gather(shard, "rows", axis=0, tiled=False).astype(BF16)

    cell, og, ng = run_cell(
        core,
        xo,
        xn,
        grad,
        rim,
        full,
        square_kernel,
        column_kernel,
    )
    return cell.transpose(1, 0, 2), og.transpose(1, 0, 2), ng.transpose(1, 0, 2)


def solution(mesh):
    rows = P(("dp", "rows"), None, None)
    in_specs = (rows, rows, rows) + (P("rows", None),) * 4 + (P(), P())
    return jax.shard_map(
        local, mesh=mesh, in_specs=in_specs, out_specs=(rows,) * 3, check_vma=False
    )
```
